128 devices in a mesh: blk: 32 (over z, x, y_lo), cols: 4 (over y_hi, core).
Axes of the slice: x: 4, y: 4 (y_hi: 2, y_lo: 2; y = y_hi * 2 + y_lo), z: 4, core: 2. Of those that a mesh axis runs over, the one named last changes fastest.
Arguments:
- focusing_plus: float32 [9728, 16, 512], P(('cols', 'blk')), may hold values from -6 to 6
- direct_field: float32 [9728, 16, 512], P(('cols', 'blk')), may hold values from -4 to 4
- reflectivity: float32 [2, 2, 9728, 9728], P(None, None, 'blk', 'cols'), may hold values from -0.0625 to 0.0625
- frequency_bins: int32 [2], replicated, may hold values from 64 to 247
- focal_onsets: int32 [16], replicated, may hold values from 32 to 191
- line_offsets: int32 [128], replicated, may hold values from 0 to 63
Outputs:
- focusing_update: float32 [9728, 16, 512], P(('cols', 'blk'))
The draws below stay inside these ranges and needn't reach their ends.
All inputs are finite; a program needn't handle non-finite values.
Results may differ from the reference program's by a relative error of at most 0.000092.
Values sent between devices are 32-bit elements; how exact they have to be, the bound alone decides.
No kernel may reach another device: no remote copies, remote signals or barrier semaphores. Data moves between devices by JAX's collectives and lax.ppermute only.
A program may use at most 64 MiB of HBM per device.

```python
import math
import jax
import jax.numpy as jnp
from jax import lax

ORDER = 9728
NT = 512
NW = 2
NF = 16
LINE = 76
LINES = 128


def set_ends(array, rng, least, largest):
    shape = array.shape
    spot = [jax.random.randint(jax.random.fold_in(rng, axis), (), 0, shape[axis]) for axis in range(len(shape))]
    array = array.at[tuple(spot)].set(least)
    longest = shape.index(max(shape))
    spot[longest] = (spot[longest] + 1) % shape[longest]
    return array.at[tuple(spot)].set(largest)


def block_scale(key, extent, split, smallest, high):
    factor_of, own = 1.0, jax.random.fold_in(key, 6)
    for dim, blocks in split:
        heights = jnp.exp(jax.random.uniform(jax.random.fold_in(own, dim), (blocks,), jnp.float32, smallest / len(split), high / len(split)))
        factor_of = factor_of * jnp.repeat(heights, extent[dim] // blocks).reshape([-1 if axis == dim else 1 for axis in range(len(extent))])
    return factor_of


def centred(key, shape, deviation, reach, split=(), kind=jnp.bfloat16):
    values = deviation * jax.random.normal(key, shape, jnp.float32)
    if split:
        values = values * block_scale(key, shape, split, -0.22, 0.18)
    return jnp.clip(values, -reach, reach).astype(kind)


def setup_inputs(seed: int = 0) -> dict:
    splits = jax.random.split(jax.random.key(seed), 7)
    return {
        "focusing_plus": centred(splits[0], (ORDER, NF, NT), 1.0, 6.0, ((0, 128),), jnp.float32),
        "direct_field": centred(splits[1], (ORDER, NF, NT), 0.5, 4.0, ((0, 128),), jnp.float32),
        "reflectivity": centred(splits[2], (NW, 2, ORDER, ORDER), ORDER ** -0.5, 0.0625, ((2, 32), (3, 4)), jnp.float32),
        "frequency_bins": jax.random.randint(splits[3], (NW,), NT // 8, NT // 2 - 8).astype(jnp.int32),
        "focal_onsets": set_ends(jax.random.randint(splits[4], (NF,), NT // 16, 3 * NT // 8), jax.random.fold_in(splits[4], 1), NT // 16, (3 * NT // 8) - 1).astype(jnp.int32),
        "line_offsets": set_ends(jax.random.randint(splits[5], (LINES,), 0, NT // 8), jax.random.fold_in(splits[5], 1), 0, (NT // 8) - 1).astype(jnp.int32),
    }


highest = lax.Precision.HIGHEST

def wave_tables(frequency_bins, samples):
    times = jnp.arange(samples, dtype=jnp.int32)
    phases = frequency_bins[:, None] * times[None, :] % samples
    angles = phases.astype(jnp.float32) * (2.0 * math.pi / samples)
    inverse = jnp.stack([jnp.cos(angles), -jnp.sin(angles)], axis=1).reshape(-1, samples)
    forward = inverse / math.sqrt(samples)
    return (forward, inverse)

def to_spectrum(signal, forward):
    positions, focal, samples = signal.shape
    flat = signal.reshape(positions * focal, samples)
    result = lax.dot_general(forward, flat, (((1,), (1,)), ((), ())), precision=highest, preferred_element_type=jnp.float32)
    return result.reshape(-1, 2, positions, focal)

def to_signal(spectrum, inverse):
    waves, halves, positions, focal = spectrum.shape
    flat = spectrum.reshape(waves * halves, positions * focal)
    result = lax.dot_general(flat, inverse, (((0,), (0,)), ((), ())), precision=highest, preferred_element_type=jnp.float32)
    return result.reshape(positions, focal, -1)

def apply_window(signal, first_row, focal_onsets, line_offsets, line_length):
    positions, focal, samples = signal.shape
    lines = lax.dynamic_slice_in_dim(line_offsets, (first_row // line_length).astype(jnp.int32), positions // line_length)
    per_row = jnp.repeat(lines, line_length)
    onsets = focal_onsets[None, :] + per_row[:, None]
    times = jnp.arange(samples, dtype=jnp.int32)
    window = (times[None, None, :] < onsets[:, :, None]) | (times[None, None, :] >= samples - onsets[:, :, None])
    return jnp.where(window, signal, jnp.zeros_like(signal))

def kernel_apply(kernel, spectrum):
    parts = jnp.einsum('wprs,wqsf->wpqrf', kernel, spectrum, precision=highest)
    real = parts[:, 0, 0] - parts[:, 1, 1]
    imag = parts[:, 0, 1] + parts[:, 1, 0]
    return jnp.stack([real, imag], axis=1)

def kernel_adjoint(kernel, spectrum):
    parts = jnp.einsum('wprs,wqrf->wpqsf', kernel, spectrum, precision=highest)
    real = parts[:, 0, 0] + parts[:, 1, 1]
    imag = parts[:, 0, 1] - parts[:, 1, 0]
    return jnp.stack([real, imag], axis=1)

def reference(focusing_plus, direct_field, reflectivity, frequency_bins, focal_onsets, line_offsets):
    samples = focusing_plus.shape[2]
    forward, inverse = wave_tables(frequency_bins, samples)
    anchor = jnp.zeros((), jnp.int32)
    plus_spectrum = to_spectrum(focusing_plus, forward)
    upgoing = kernel_apply(reflectivity, plus_spectrum)
    focusing_minus = apply_window(to_signal(upgoing, inverse), anchor, focal_onsets, line_offsets, LINE)
    minus_spectrum = to_spectrum(focusing_minus, forward)
    adjoint = kernel_adjoint(reflectivity, minus_spectrum)
    correction = apply_window(to_signal(adjoint, inverse), anchor, focal_onsets, line_offsets, LINE)
    return direct_field - correction
```

```python
import math

import jax
import jax.numpy as jnp
from jax import lax
from jax.sharding import PartitionSpec as P

LINE = 76


highest = lax.Precision.HIGHEST
high = lax.Precision.HIGH


def wave_tables(frequency_bins, samples):
    times = jnp.arange(samples, dtype=jnp.int32)
    phases = frequency_bins[:, None] * times[None, :] % samples
    angles = phases.astype(jnp.float32) * (2.0 * math.pi / samples)
    inverse = jnp.stack([jnp.cos(angles), -jnp.sin(angles)], axis=1).reshape(-1, samples)
    forward = inverse / math.sqrt(samples)
    return (forward, inverse)


def windows(onsets, samples):
    times = jnp.arange(samples, dtype=jnp.int32)
    return (times < onsets[..., None]) | (times >= samples - onsets[..., None])


def local(focusing_plus, direct_field, reflectivity, frequency_bins, focal_onsets, line_offsets):
    own, focal, samples = focusing_plus.shape
    waves, _, block_rows, group_columns = reflectivity.shape
    parts = 2 * waves
    blocks = group_columns // own
    block_index = lax.axis_index("blk")
    group_index = lax.axis_index("cols")
    forward, inverse = wave_tables(frequency_bins, samples)

    spectrum = lax.dot_general(
        focusing_plus, forward, (((2,), (1,)), ((), ())), precision=high
    )
    spectrum = spectrum.transpose(0, 2, 1).reshape(own, parts * focal)
    width = parts * focal
    packed = spectrum.reshape(own * width // 128, 128)
    gathered = lax.all_to_all(
        jnp.broadcast_to(packed[None], (blocks,) + packed.shape), "blk", 0, 0
    )
    field = gathered.reshape(group_columns, waves, 2, focal)

    grown = jnp.einsum("wprs,swqf->wprqf", reflectivity, field, precision=high)
    real = grown[:, 0, :, 0] - grown[:, 1, :, 1]
    imag = grown[:, 0, :, 1] + grown[:, 1, :, 0]
    partial_value = jnp.stack([real, imag], axis=1)
    partial_value = partial_value.transpose(2, 0, 1, 3).reshape(-1, 128)
    shares = lax.all_gather(partial_value, "cols", axis=0)
    upgoing = shares.sum(0).reshape(block_rows // LINE, LINE, parts, focal)

    lines = lax.dynamic_slice_in_dim(line_offsets, block_index * (block_rows // LINE), block_rows // LINE)
    window = windows(lines[:, None] + focal_onsets[None, :], samples).astype(jnp.float32)
    pairs = (forward[:, None, :] * inverse[None, :, :]).reshape(parts * parts, samples)
    mixing = lax.dot_general(
        window.reshape(-1, samples), pairs, (((1,), (1,)), ((), ())), precision=highest
    ).reshape(block_rows // LINE, focal, parts, parts)
    minus = [
        sum(mixing[:, None, :, a, b] * upgoing[:, :, b] for b in range(parts))
        for a in range(parts)
    ]
    minus = jnp.stack(minus, axis=2).reshape(block_rows, waves, 2, focal)

    back = jnp.einsum("wprs,rwqf->swpqf", reflectivity, minus, precision=high)
    real = back[:, :, 0, 0] + back[:, :, 1, 1]
    imag = back[:, :, 0, 1] - back[:, :, 1, 0]
    adjoint = jnp.stack([real, imag], axis=2).reshape(blocks, own * width // 128, 128)
    scattered = lax.all_to_all(adjoint, "blk", 0, 0)
    update = scattered.sum(0).reshape(own, parts, focal)

    first_source = group_index * group_columns + block_index * own
    line = lax.dynamic_slice_in_dim(line_offsets, first_source // LINE, own // LINE)
    window = windows(jnp.repeat(line, LINE)[:, None] + focal_onsets[None, :], samples)
    signal = lax.dot_general(
        update, inverse, (((1,), (0,)), ((), ())), precision=high
    )
    return direct_field - jnp.where(window, signal, 0.0)


def solution(mesh):
    return jax.shard_map(
        local,
        mesh=mesh,
        in_specs=(
            P(("cols", "blk"), None, None),
            P(("cols", "blk"), None, None),
            P(None, None, "blk", "cols"),
            P(),
            P(),
            P(),
        ),
        out_specs=P(("cols", "blk"), None, None),
        check_vma=False,
    )
```

```python
import functools
import math

import jax
import jax.numpy as jnp
from jax import lax
from jax.experimental import pallas as pl
from jax.experimental.pallas import tpu as pltpu
from jax.sharding import PartitionSpec as P

LINE = 76
LANES = 128
HALF = 64
FOCAL = 16
PARTS = 4

VMEM = pl.BlockSpec(memory_space=pltpu.VMEM)
SMEM = pl.BlockSpec(memory_space=pltpu.SMEM)
ANY = pl.BlockSpec(memory_space=pl.ANY)
NT = (((1,), (1,)), ((), ()))
NN = (((1,), (0,)), ((), ()))
f32 = jnp.float32
bf16 = jnp.bfloat16


def dot(a, b, dims=NN, precision=None):
    return lax.dot_general(a, b, dims, precision=precision, preferred_element_type=f32)


def iota(shape, dim):
    return lax.broadcasted_iota(jnp.int32, shape, dim)


def rest_of(x):
    return x - x.astype(bf16).astype(f32)


def waves_of(bins, rows, samples, shift=0):
    shape = (rows, samples)
    part = (iota(shape, 0) + shift) & 3
    step = jnp.where(part < 2, bins[0], bins[1])
    phase = (step * iota(shape, 1) + (samples // 4) * (part & 1)) & (samples - 1)
    return jnp.cos(phase.astype(f32) * (2.0 * math.pi / samples))


def repeated(rows, times):
    one = jnp.concatenate(
        [jnp.broadcast_to(rows[k : k + 1], (FOCAL, rows.shape[1])) for k in range(PARTS)], 0
    )
    return jnp.concatenate([one] * times, 0) if times > 1 else one


def spectrum_kernel(
    chunks, bins_in, signal, kernel, out, early, bins, held, table, wide, sems, bins_sem, early_sem
):
    own, focal, samples = held.shape
    fetch = pltpu.make_async_copy(bins_in, bins, bins_sem)
    fetch.start()
    copies = []
    for i, (lo, hi) in enumerate(chunks):
        copies.append(
            pltpu.make_async_copy(signal.at[lo:hi], held.at[lo:hi], sems.at[i])
        )
        copies[-1].start()
    ahead = pltpu.make_async_copy(kernel.at[: early.shape[0]], early, early_sem)
    ahead.start()
    fetch.wait()
    forward = waves_of(bins, 8, samples) * (1.0 / math.sqrt(samples))
    table[0:HALF] = repeated(forward, 1).astype(bf16)
    table[HALF:LANES] = repeated(rest_of(forward), 1).astype(bf16)
    both = table[...]
    for (lo, hi), copy in zip(chunks, copies):
        copy.wait()
        x = held[lo:hi].reshape((hi - lo) * focal, samples)
        wide[lo * focal : hi * focal] = dot(x.astype(bf16), both, NT) + dot(
            rest_of(x).astype(bf16), both, NT
        )
    lane = iota((own, LANES), 1)
    total = jnp.zeros((own, LANES), f32)
    for f in range(focal):
        total = jnp.where((lane & 15) == f, wide[pl.ds(f, own, stride=focal), :], total)
    total = total + pltpu.roll(total, HALF, 1)
    half = own // 2
    packed = jnp.where(lane[:half] < HALF, total[:half], total[half:])
    out[...] = jnp.broadcast_to(packed[None], out.shape)
    ahead.wait()


def tables_kernel(axes, bins, focal_onsets, line_offsets, mixing, last):
    samples = last.shape[1]
    lines = mixing.shape[1]
    block = lax.axis_index(axes[0])
    group = lax.axis_index(axes[1])
    forward = waves_of(bins, 8, samples) * (1.0 / math.sqrt(samples))
    row = iota((FOCAL, samples), 0)
    time = iota((FOCAL, samples), 1)
    focal = jnp.zeros((FOCAL, samples), jnp.int32)
    for f in range(FOCAL):
        focal = jnp.where(row == f, focal_onsets[f], focal)

    def window(line):
        onset = focal + line_offsets[line]
        return jnp.where((time < onset) | (time >= samples - onset), 1.0, 0.0)

    shape = (lines * FOCAL, LANES)
    inside = jnp.concatenate([window(block * lines + l) for l in range(lines)], 0)
    same = (iota(shape, 0) & 15) == (iota(shape, 1) & 15)
    for d in range(PARTS):
        pair = repeated(forward * waves_of(bins, 8, samples, d), 2)
        value = jnp.where(same, dot(inside, pair, NT, lax.Precision.HIGHEST), 0.0)
        for l in range(lines):
            mixing[d, l : l + 1] = jnp.sum(
                value[l * FOCAL : (l + 1) * FOCAL], axis=0, keepdims=True
            )
    own = window(group * (line_offsets.shape[0] // 4) + block)
    inverse = repeated(waves_of(bins, 8, samples), 1) * jnp.concatenate([own] * PARTS, 0)
    high, low = inverse.astype(bf16), rest_of(inverse).astype(bf16)
    last[0:64] = high
    last[64:128] = high
    last[128:192] = low
    last[192:256] = low


def apply_kernel(chunks, field, early, kernel, out, high, low, late, rows, right, sems):
    first = early.shape[0]
    copies = {}
    for lo, hi in chunks:
        if lo >= first:
            copies[lo] = pltpu.make_async_copy(
                kernel.at[lo:hi], late.at[lo - first : hi - first], sems.at[len(copies)]
            )
            copies[lo].start()
    blocks, half, _ = field.shape
    lane = iota((half, LANES), 1)
    for b in range(blocks):
        x = field[b]
        turned = pltpu.roll(x, HALF, 1)
        rows[2 * half * b : 2 * half * b + half] = jnp.where(lane < HALF, x, turned)
        rows[2 * half * b + half : 2 * half * (b + 1)] = jnp.where(lane < HALF, turned, x)
    x = rows[...]
    right[...] = jnp.where(iota(x.shape, 1) < HALF, x, rest_of(x)).astype(bf16)
    count = high.shape[0] // PARTS
    terms = []
    for lo, hi in chunks:
        if lo < first:
            x = early[lo:hi]
        else:
            copies[lo].wait()
            x = late[lo - first : hi - first]
        upper, lower = x.astype(bf16), rest_of(x).astype(bf16)
        high[lo:hi] = upper
        low[lo:hi] = lower
        terms.append(dot(upper, right[...]) + dot(lower, right[...]))
    total = jnp.concatenate(terms, 0)
    lane = iota((count, LANES), 1)
    grown = []
    for w in range(2):
        parts = []
        for p in range(2):
            x = total[(2 * w + p) * count : (2 * w + p + 1) * count]
            parts.append(x + pltpu.roll(x, HALF, 1))
        real, imag = parts
        crossed = jnp.where(
            (lane & 16) == 0, -pltpu.roll(imag, LANES - 16, 1), pltpu.roll(imag, 16, 1)
        )
        grown.append(real + crossed)
    value = jnp.where((lane & 32) == 0, grown[0], grown[1])
    out[...] = jnp.where(lane[: count // 2] < HALF, value[: count // 2], value[count // 2 :])


def adjoint_kernel(one, other, mixing, high, low, out, flat, rows):
    count = high.shape[0] // PARTS
    x = one[...] + other[...]
    turned = pltpu.roll(x, HALF, 1)
    lane = iota(x.shape, 1)
    x = jnp.concatenate([jnp.where(lane < HALF, x, turned), jnp.where(lane < HALF, turned, x)], 0)
    row = iota(x.shape, 0)
    minus = jnp.zeros_like(x)
    for d in range(PARTS):
        weight = jnp.broadcast_to(mixing[d, 0:1], x.shape)
        for l in range(1, count // LINE):
            weight = jnp.where(row >= l * LINE, mixing[d, l : l + 1], weight)
        minus = minus + weight * (x if d == 0 else pltpu.roll(x, LANES - 16 * d, 1))
    minus = minus.T[:HALF]
    upper, lower = minus.astype(bf16), rest_of(minus).astype(bf16)
    for w in range(2):
        at = 32 * w
        total = None
        for p in range(2):
            if p == 0:
                left = [upper[at : at + 32], lower[at : at + 32]]
            else:
                left = []
                for v in (upper, lower):
                    left += [v[at + 16 : at + 32], -v[at : at + 16]]
            left = jnp.concatenate(left, 0)
            base = (2 * w + p) * count
            term = dot(left, high[base : base + count]) + dot(left, low[base : base + count])
            total = term if total is None else total + term
        flat[at : at + 32] = total[:32] + total[32:]
    columns = flat.shape[1]
    for j in range(columns // LANES):
        block = flat[:, j * LANES : (j + 1) * LANES]
        rows[j * LANES : (j + 1) * LANES] = jnp.concatenate([block, block], 0).T
    blocks, half, _ = out.shape
    lane = iota((half, LANES), 1)
    for b in range(blocks):
        at = 2 * half * b
        out[b] = jnp.where(lane < HALF, rows[at : at + half], rows[at + half : at + 2 * half])


def signal_kernel(chunks, pieces, last, direct, out, done, update, wide, out_sems):
    own, focal, samples = done.shape
    total = pieces[0]
    for b in range(1, pieces.shape[0]):
        total = total + pieces[b]
    turned = pltpu.roll(total, HALF, 1)
    half = own // 2
    lane = iota((half, LANES), 1)
    update[:half] = jnp.where(lane < HALF, total, turned)
    update[half:] = jnp.where(lane < HALF, turned, total)
    x = update[...]
    lane = iota(x.shape, 1)
    x = jnp.where(lane < HALF, x, rest_of(x))
    for f in range(focal):
        wide[pl.ds(f, own, stride=focal), :] = jnp.where((lane & 15) == f, x, 0.0)
    backs = []
    for i, (lo, hi) in enumerate(chunks):
        left = wide[lo * focal : hi * focal].astype(bf16)
        value = dot(jnp.concatenate([left, left], 1), last[...])
        done[lo:hi] = direct[lo:hi] - value.reshape(hi - lo, focal, samples)
        backs.append(pltpu.make_async_copy(done.at[lo:hi], out.at[lo:hi], out_sems.at[i]))
        backs[-1].start()
    for copy in backs:
        copy.wait()


def call(kernel, outs, ins, out_specs, scratch=(), cost=0, grid=None, limit=32):
    kwargs = {} if grid is None else dict(grid=grid)
    return pl.pallas_call(
        kernel,
        out_shape=outs,
        in_specs=ins,
        out_specs=out_specs,
        scratch_shapes=list(scratch),
        compiler_params=pltpu.CompilerParams(vmem_limit_bytes=limit << 20),
        cost_estimate=pl.CostEstimate(flops=cost, bytes_accessed=cost, transcendentals=0),
        **kwargs,
    )


def local(focusing_plus, direct_field, reflectivity, frequency_bins, focal_onsets, line_offsets):
    own, focal, samples = focusing_plus.shape
    waves, _, block_rows, columns = reflectivity.shape
    blocks = columns // own
    half = own // 2
    lines = block_rows // LINE
    assert (waves, focal, own) == (2, FOCAL, LINE)
    chunks = [(0, 16), (16, 40), (40, 64), (64, own)]
    shape = jax.ShapeDtypeStruct
    far = functools.partial(pltpu.with_memory_space_constraint, memory_space=pltpu.HBM)

    kernel = reflectivity.reshape(PARTS * block_rows, columns)
    first = 2 * block_rows
    copies, early = call(
        functools.partial(spectrum_kernel, chunks),
        [shape((blocks, half, LANES), f32), pltpu.VMEM((first, columns), f32)],
        [ANY, ANY, ANY],
        [VMEM, VMEM],
        [
            pltpu.SMEM(frequency_bins.shape, jnp.int32),
            pltpu.VMEM((own, focal, samples), f32),
            pltpu.VMEM((LANES, samples), bf16),
            pltpu.VMEM((own * focal, LANES), f32),
            pltpu.SemaphoreType.DMA((len(chunks),)),
            pltpu.SemaphoreType.DMA,
            pltpu.SemaphoreType.DMA,
        ],
        limit=24,
    )(far(frequency_bins), far(focusing_plus), far(kernel))
    field = lax.all_to_all(copies, "blk", 0, 0)

    mixing, last = call(
        functools.partial(tables_kernel, ("blk", "cols")),
        [shape((PARTS, lines, LANES), f32), shape((4 * HALF, samples), bf16)],
        [SMEM, SMEM, SMEM],
        [VMEM, VMEM],
        cost=1 << 20,
    )(frequency_bins, focal_onsets, line_offsets)

    cut = block_rows // 32 * 16
    pieces_of = [
        (p * block_rows + lo, p * block_rows + hi)
        for p in range(PARTS)
        for lo, hi in ((0, cut), (cut, block_rows))
    ]
    value, high, low = call(
        functools.partial(apply_kernel, pieces_of),
        [shape((block_rows // 2, LANES), f32)] + [pltpu.VMEM(kernel.shape, bf16)] * 2,
        [VMEM, VMEM, ANY],
        [VMEM] * 3,
        [
            pltpu.VMEM((kernel.shape[0] - first, columns), f32),
            pltpu.VMEM((columns, LANES), f32),
            pltpu.VMEM((columns, LANES), bf16),
            pltpu.SemaphoreType.DMA((len(pieces_of) // 2,)),
        ],
        limit=24,
    )(field, early, far(kernel))
    value = value + lax.ppermute(value, "cols", [(0, 1), (1, 0), (2, 3), (3, 2)])
    other = lax.ppermute(value, "cols", [(0, 2), (2, 0), (1, 3), (3, 1)])

    partial_update = call(
        adjoint_kernel,
        shape((blocks, half, LANES), f32),
        [VMEM] * 5,
        VMEM,
        [pltpu.VMEM((HALF, columns), f32), pltpu.VMEM((columns, LANES), f32)],
    )(value, other, mixing, high, low)
    pieces = lax.all_to_all(partial_update, "blk", 0, 0)

    return call(
        functools.partial(signal_kernel, chunks),
        shape((own, focal, samples), f32),
        [VMEM, VMEM, VMEM],
        ANY,
        [
            pltpu.VMEM((own, focal, samples), f32),
            pltpu.VMEM((own, LANES), f32),
            pltpu.VMEM((own * focal, LANES), f32),
            pltpu.SemaphoreType.DMA((len(chunks),)),
        ],
    )(pieces, last, direct_field)


def solution(mesh):
    return jax.shard_map(
        local,
        mesh=mesh,
        in_specs=(
            P(("cols", "blk"), None, None),
            P(("cols", "blk"), None, None),
            P(None, None, "blk", "cols"),
            P(),
            P(),
            P(),
        ),
        out_specs=P(("cols", "blk"), None, None),
        check_vma=False,
    )
```

```python
import functools
import math

import jax
import jax.numpy as jnp
from jax import lax
from jax.experimental import pallas as pl
from jax.experimental.pallas import tpu as pltpu
from jax.sharding import PartitionSpec as P

LINE = 76
LANES = 128
HALF = 64
FOCAL = 16
PARTS = 4
SPAN = 512
DSPAN = 1280

VMEM = pl.BlockSpec(memory_space=pltpu.VMEM)
SMEM = pl.BlockSpec(memory_space=pltpu.SMEM)
ANY = pl.BlockSpec(memory_space=pl.ANY)
NT = (((1,), (1,)), ((), ()))
NN = (((1,), (0,)), ((), ()))
f32 = jnp.float32
bf16 = jnp.bfloat16


def dot(a, b, dims=NN, precision=None):
    return lax.dot_general(a, b, dims, precision=precision, preferred_element_type=f32)


def iota(shape, dim):
    return lax.broadcasted_iota(jnp.int32, shape, dim)


def rest_of(x):
    return x - x.astype(bf16).astype(f32)


def waves_of(bins, rows, samples, shift=0):
    shape = (rows, samples)
    part = (iota(shape, 0) + shift) & 3
    step = jnp.where(part < 2, bins[0], bins[1])
    phase = (step * iota(shape, 1) + (samples // 4) * (part & 1)) & (samples - 1)
    return jnp.cos(phase.astype(f32) * (2.0 * math.pi / samples))


def repeated(rows, times):
    one = jnp.concatenate(
        [jnp.broadcast_to(rows[k : k + 1], (FOCAL, rows.shape[1])) for k in range(PARTS)], 0
    )
    return jnp.concatenate([one] * times, 0) if times > 1 else one


def spectrum_kernel(chunks, bins_in, signal, wide, bins, held, table, sems, bins_sem):
    _, focal, samples = held.shape
    fetch = pltpu.make_async_copy(bins_in, bins, bins_sem)
    fetch.start()
    copies = []
    for i, (lo, hi) in enumerate(chunks):
        copies.append(
            pltpu.make_async_copy(signal.at[lo:hi], held.at[lo:hi], sems.at[i])
        )
        copies[-1].start()
    fetch.wait()
    forward = waves_of(bins, 8, samples) * (1.0 / math.sqrt(samples))
    table[0:HALF] = repeated(forward, 1).astype(bf16)
    table[HALF:LANES] = repeated(rest_of(forward), 1).astype(bf16)
    both = table[...]
    for (lo, hi), copy in zip(chunks, copies):
        copy.wait()
        x = held[lo:hi].reshape((hi - lo) * focal, samples)
        rounded = x.astype(bf16)
        wide[lo * focal : hi * focal] = dot(rounded, both, NT) + dot(
            (x - rounded.astype(f32)).astype(bf16), both, NT
        )


def pack_kernel(wide, _, out):
    own = 2 * out.shape[1]
    lane = iota((own, LANES), 1)
    total = jnp.zeros((own, LANES), f32)
    for f in range(FOCAL):
        total = jnp.where((lane & 15) == f, wide[pl.ds(f, own, stride=FOCAL), :], total)
    total = total + pltpu.roll(total, HALF, 1)
    half = own // 2
    packed = jnp.where(lane[:half] < HALF, total[:half], total[half:])
    out[...] = jnp.broadcast_to(packed[None], out.shape)


def tables_kernel(axes, bins, focal_onsets, line_offsets, mixing, last):
    samples = last.shape[1]
    lines = mixing.shape[2] // LINE
    block = lax.axis_index(axes[0])
    group = lax.axis_index(axes[1])
    forward = waves_of(bins, 8, samples) * (1.0 / math.sqrt(samples))
    row = iota((FOCAL, samples), 0)
    time = iota((FOCAL, samples), 1)
    focal = jnp.zeros((FOCAL, samples), jnp.int32)
    for f in range(FOCAL):
        focal = jnp.where(row == f, focal_onsets[f], focal)

    def window(line):
        onset = focal + line_offsets[line]
        return jnp.where((time < onset) | (time >= samples - onset), 1.0, 0.0)

    inside = jnp.concatenate([window(block * lines + l) for l in range(lines)], 0)
    rows = lines * FOCAL
    count = mixing.shape[2]
    same = (iota((HALF, rows), 0) & 15) == (iota((HALF, rows), 1) & 15)
    first = (iota((rows, count), 0) >> 4) * LINE
    column = iota((rows, count), 1)
    spread = jnp.where((column >= first) & (column < first + LINE), 1.0, 0.0)
    for d in range(PARTS):
        pair = repeated(forward * waves_of(bins, 8, samples, d), 1)
        value = jnp.where(same, dot(pair, inside, NT, lax.Precision.HIGHEST), 0.0)
        mixing[d] = dot(value, spread, NN, lax.Precision.HIGHEST)
    own = window(group * (line_offsets.shape[0] // 4) + block)
    inverse = repeated(waves_of(bins, 8, samples), 1) * jnp.concatenate([own] * PARTS, 0)
    high, low = inverse.astype(bf16), rest_of(inverse).astype(bf16)
    last[0:64] = high
    last[64:128] = high
    last[128:192] = low
    last[192:256] = low


def apply_kernel(order, field, kernel, out, high, low, rows, left, sums):
    blocks, half, _ = field.shape
    columns = left.shape[1]
    count = high.shape[0] // PARTS
    spans = [slice(lo, min(lo + SPAN, columns)) for lo in range(0, columns, SPAN)]
    units = [(span, k) for span in spans for k in range(PARTS)]
    ready = [0]

    def prepare(span):
        lane = iota((half, LANES), 1)
        while ready[0] * 2 * half < span.stop:
            b = ready[0]
            x = field[order.index(b)]
            turned = pltpu.roll(x, HALF, 1)
            rows[2 * half * b : 2 * half * b + half] = jnp.where(lane < HALF, x, turned)
            rows[2 * half * b + half : 2 * half * (b + 1)] = jnp.where(lane < HALF, turned, x)
            ready[0] += 1
        lane = iota((LANES, LANES), 1)
        for j in range(span.start, span.stop, LANES):
            x = rows[j : j + LANES]
            left[:, j : j + LANES] = jnp.where(lane < HALF, x, rest_of(x)).T.astype(bf16)

    def split(span, k):
        for c in range(0, count, 16):
            at = slice(k * count + c, k * count + c + 16)
            x = kernel[k // 2, k % 2, c : c + 16, span]
            high[at, span] = x.astype(bf16)
            x = x - high[at, span].astype(f32)
            low[at, span] = x.astype(bf16)

    split(*units[0])
    prepare(spans[0])
    for i, (span, k) in enumerate(units):
        at = slice(k * count, (k + 1) * count)
        w = 32 * (k // 2)
        upper = left[w : w + 32, span]
        both = jnp.concatenate([upper, left[HALF + w : HALF + w + 32, span]], 0)
        x = dot(both, high[at, span], NT)
        x = x[:32] + x[32:] + dot(upper, low[at, span], NT)
        sums[k] = x if span.start == 0 else sums[k] + x
        if i + 1 < len(units):
            split(*units[i + 1])
            if units[i + 1][0] is not span:
                prepare(units[i + 1][0])
    for w in range(2):
        real, imag = sums[2 * w], sums[2 * w + 1]
        out[32 * w : 32 * w + 16] = real[:16] - imag[16:]
        out[32 * w + 16 : 32 * w + 32] = real[16:] + imag[:16]


def adjoint_kernel(order, one, other, mixing, high, low, out, flat, rows):
    count = high.shape[0] // PARTS
    x = one[...] + other[...]
    minus = mixing[0] * x
    for d in range(1, PARTS):
        at = FOCAL * d
        minus = minus + mixing[d] * jnp.concatenate([x[at:], x[:at]], 0)
    upper, lower = minus.astype(bf16), rest_of(minus).astype(bf16)
    columns = flat.shape[1]
    lefts = []
    for w in range(2):
        at = 32 * w
        lefts.append(jnp.concatenate([upper[at : at + 32], lower[at : at + 32]], 0))
        left = []
        for v in (upper, lower):
            left += [v[at + 16 : at + 32], -v[at : at + 16]]
        lefts.append(jnp.concatenate(left, 0))
    for lo in range(0, columns, DSPAN):
        at = slice(lo, min(lo + DSPAN, columns))
        for w in range(2):
            total = None
            for p in range(2):
                left = lefts[2 * w + p]
                base = (2 * w + p) * count
                term = dot(left, high[base : base + count, at])
                term = term[:32] + term[32:] + dot(left[:32], low[base : base + count, at])
                total = term if total is None else total + term
            flat[32 * w : 32 * w + 32, at] = total
        for j in range(at.start, at.stop, LANES):
            block = flat[:, j : j + LANES]
            rows[j : j + LANES] = jnp.concatenate([block, block], 0).T
    blocks, half, _ = out.shape
    lane = iota((half, LANES), 1)
    for b in range(blocks):
        at = 2 * half * b
        out[order.index(b)] = jnp.where(lane < HALF, rows[at : at + half], rows[at + half : at + 2 * half])


def signal_kernel(chunks, pieces, last, direct, out, done, update, wide, out_sems):
    own, focal, samples = done.shape
    total = pieces[0]
    for b in range(1, pieces.shape[0]):
        total = total + pieces[b]
    turned = pltpu.roll(total, HALF, 1)
    half = own // 2
    lane = iota((half, LANES), 1)
    update[:half] = jnp.where(lane < HALF, total, turned)
    update[half:] = jnp.where(lane < HALF, turned, total)
    x = update[...]
    lane = iota(x.shape, 1)
    x = jnp.where(lane < HALF, x, rest_of(x))
    for f in range(focal):
        wide[pl.ds(f, own, stride=focal), :] = jnp.where((lane & 15) == f, x, 0.0)
    backs = []
    for i, (lo, hi) in enumerate(chunks):
        left = wide[lo * focal : hi * focal].astype(bf16)
        value = dot(jnp.concatenate([left, left], 1), last[...])
        done[lo:hi] = direct[lo:hi] - value.reshape(hi - lo, focal, samples)
        backs.append(pltpu.make_async_copy(done.at[lo:hi], out.at[lo:hi], out_sems.at[i]))
        backs[-1].start()
    for copy in backs:
        copy.wait()


def members():
    return [(9 * i) % 32 for i in range(32)]


def call(kernel, outs, ins, out_specs, scratch=(), cost=0, grid=None, limit=32):
    kwargs = {} if grid is None else dict(grid=grid)
    return pl.pallas_call(
        kernel,
        out_shape=outs,
        in_specs=ins,
        out_specs=out_specs,
        scratch_shapes=list(scratch),
        compiler_params=pltpu.CompilerParams(vmem_limit_bytes=limit << 20),
        cost_estimate=pl.CostEstimate(flops=cost, bytes_accessed=cost, transcendentals=0),
        **kwargs,
    )


def local(focusing_plus, direct_field, reflectivity, frequency_bins, focal_onsets, line_offsets):
    own, focal, samples = focusing_plus.shape
    waves, _, block_rows, columns = reflectivity.shape
    blocks = columns // own
    half = own // 2
    lines = block_rows // LINE
    assert (waves, focal, own) == (2, FOCAL, LINE)
    chunks = [(0, 16), (16, 40), (40, 64), (64, own)]
    early = [(0, 48), (48, own)]
    order = members()
    assert sorted(order) == list(range(blocks))
    exchange = functools.partial(
        lax.all_to_all,
        axis_name="blk",
        split_axis=0,
        concat_axis=0,
        tiled=True,
        axis_index_groups=[order],
    )
    shape = jax.ShapeDtypeStruct
    far = functools.partial(pltpu.with_memory_space_constraint, memory_space=pltpu.HBM)

    wide = call(
        functools.partial(spectrum_kernel, early),
        pltpu.VMEM((own * focal, LANES), f32),
        [ANY, ANY],
        VMEM,
        [
            pltpu.SMEM(frequency_bins.shape, jnp.int32),
            pltpu.VMEM((own, focal, samples), f32),
            pltpu.VMEM((LANES, samples), bf16),
            pltpu.SemaphoreType.DMA((len(early),)),
            pltpu.SemaphoreType.DMA,
        ],
        limit=16,
    )(far(frequency_bins), far(focusing_plus))
    copies = call(
        pack_kernel,
        shape((blocks, half, LANES), f32),
        [VMEM, ANY],
        VMEM,
        limit=16,
    )(wide, far(reflectivity))
    field = exchange(copies)

    mixing, last = call(
        functools.partial(tables_kernel, ("blk", "cols")),
        [shape((PARTS, HALF, block_rows), f32), shape((4 * HALF, samples), bf16)],
        [SMEM, SMEM, SMEM],
        [VMEM, VMEM],
        cost=1 << 20,
    )(frequency_bins, focal_onsets, line_offsets)

    value, high, low = call(
        functools.partial(apply_kernel, order),
        [shape((HALF, block_rows), f32)] + [pltpu.VMEM((PARTS * block_rows, columns), bf16)] * 2,
        [VMEM, VMEM],
        [VMEM] * 3,
        [
            pltpu.VMEM((columns, LANES), f32),
            pltpu.VMEM((LANES, columns), bf16),
            pltpu.VMEM((PARTS, 32, block_rows), f32),
        ],
        limit=16,
    )(field, reflectivity)
    value = value + lax.ppermute(value, "cols", [(0, 1), (1, 0), (2, 3), (3, 2)])
    other = lax.ppermute(value, "cols", [(0, 2), (2, 0), (1, 3), (3, 1)])

    partial_update = call(
        functools.partial(adjoint_kernel, order),
        shape((blocks, half, LANES), f32),
        [VMEM] * 5,
        VMEM,
        [pltpu.VMEM((HALF, columns), f32), pltpu.VMEM((columns, LANES), f32)],
    )(value, other, mixing, high, low)
    pieces = exchange(partial_update)

    return call(
        functools.partial(signal_kernel, chunks),
        shape((own, focal, samples), f32),
        [VMEM, VMEM, VMEM],
        ANY,
        [
            pltpu.VMEM((own, focal, samples), f32),
            pltpu.VMEM((own, LANES), f32),
            pltpu.VMEM((own * focal, LANES), f32),
            pltpu.SemaphoreType.DMA((len(chunks),)),
        ],
    )(pieces, last, direct_field)


def solution(mesh):
    return jax.shard_map(
        local,
        mesh=mesh,
        in_specs=(
            P(("cols", "blk"), None, None),
            P(("cols", "blk"), None, None),
            P(None, None, "blk", "cols"),
            P(),
            P(),
            P(),
        ),
        out_specs=P(("cols", "blk"), None, None),
        check_vma=False,
    )
```

```python
import functools
import math

import jax
import jax.numpy as jnp
from jax import lax
from jax.experimental import pallas as pl
from jax.experimental.pallas import tpu as pltpu
from jax.sharding import PartitionSpec as P

LINE = 76
LANES = 128
HALF = 64
FOCAL = 16
PARTS = 4
SPAN = 512
DSPAN = 1280

VMEM = pl.BlockSpec(memory_space=pltpu.VMEM)
SMEM = pl.BlockSpec(memory_space=pltpu.SMEM)
ANY = pl.BlockSpec(memory_space=pl.ANY)
NT = (((1,), (1,)), ((), ()))
NN = (((1,), (0,)), ((), ()))
f32 = jnp.float32
bf16 = jnp.bfloat16


def dot(a, b, dims=NN, precision=None):
    return lax.dot_general(a, b, dims, precision=precision, preferred_element_type=f32)


def iota(shape, dim):
    return lax.broadcasted_iota(jnp.int32, shape, dim)


def rest_of(x):
    return x - x.astype(bf16).astype(f32)


def waves_of(bins, rows, samples, shift=0):
    shape = (rows, samples)
    part = (iota(shape, 0) + shift) & 3
    step = jnp.where(part < 2, bins[0], bins[1])
    phase = (step * iota(shape, 1) + (samples // 4) * (part & 1)) & (samples - 1)
    return jnp.cos(phase.astype(f32) * (2.0 * math.pi / samples))


def repeated(rows, times):
    one = jnp.concatenate(
        [jnp.broadcast_to(rows[k : k + 1], (FOCAL, rows.shape[1])) for k in range(PARTS)], 0
    )
    return jnp.concatenate([one] * times, 0) if times > 1 else one


def fill_tables(axes, waves, bins, focal_onsets, line_offsets, mixing, last):
    samples = last.shape[1]
    lines = mixing.shape[2] // LINE
    block = lax.axis_index(axes[0])
    group = lax.axis_index(axes[1])
    row = iota((FOCAL, samples), 0)
    time = iota((FOCAL, samples), 1)
    focal = jnp.zeros((FOCAL, samples), jnp.int32)
    for f in range(FOCAL):
        focal = jnp.where(row == f, focal_onsets[f], focal)

    def window(line):
        onset = focal + line_offsets[line]
        return jnp.where((time < onset) | (time >= samples - onset), 1.0, 0.0)

    inside = jnp.concatenate([window(block * lines + l) for l in range(lines)], 0).astype(bf16)
    rows = lines * FOCAL
    count = mixing.shape[2]
    same = (iota((HALF, rows), 0) & 15) == (iota((HALF, rows), 1) & 15)
    first = (iota((rows, count), 0) >> 4) * LINE
    column = iota((rows, count), 1)
    spread = jnp.where((column >= first) & (column < first + LINE), 1.0, 0.0).astype(bf16)
    forward = waves * (1.0 / math.sqrt(samples))
    for d in range(PARTS):
        pair = forward * waves_of(bins, 8, samples, d)
        value = dot(repeated(pair, 1).astype(bf16), inside, NT) + dot(
            repeated(rest_of(pair), 1).astype(bf16), inside, NT
        )
        value = jnp.where(same, value, 0.0)
        mixing[d] = dot(value.astype(bf16), spread) + dot(rest_of(value).astype(bf16), spread)
    own = window(group * (line_offsets.shape[0] // 4) + block)
    inverse = repeated(waves, 1) * jnp.concatenate([own] * PARTS, 0)
    high, low = inverse.astype(bf16), rest_of(inverse).astype(bf16)
    last[0:64] = high
    last[64:128] = high
    last[128:192] = low
    last[192:256] = low


def spectrum_kernel(
    axes, bins_in, focal_in, lines_in, signal, wide, mixing, last,
    bins, focal_onsets, line_offsets, held, table, sem, sems,
):
    own, focal, samples = held.shape
    fetches = []
    for i, (source, target) in enumerate(
        [(bins_in, bins), (focal_in, focal_onsets), (lines_in, line_offsets)]
    ):
        fetches.append(pltpu.make_async_copy(source, target, sems.at[i]))
        fetches[-1].start()
    copy = pltpu.make_async_copy(signal, held, sem)
    copy.start()
    for fetch in fetches:
        fetch.wait()
    waves = waves_of(bins, 8, samples)
    forward = waves * (1.0 / math.sqrt(samples))
    table[...] = jnp.concatenate(
        [repeated(forward, 1), repeated(rest_of(forward), 1)], 0
    ).T.astype(bf16)
    fill_tables(axes, waves, bins, focal_onsets, line_offsets, mixing, last)
    both = table[...]
    copy.wait()
    x = held[...].reshape(own * focal, samples)
    rounded = x.astype(bf16)
    wide[...] = dot(rounded, both) + dot((x - rounded.astype(f32)).astype(bf16), both)


def pack_kernel(wide, _, out):
    own = 2 * out.shape[1]
    lane = iota((own, LANES), 1)
    total = jnp.zeros((own, LANES), f32)
    for f in range(FOCAL):
        total = jnp.where((lane & 15) == f, wide[pl.ds(f, own, stride=FOCAL), :], total)
    total = total + pltpu.roll(total, HALF, 1)
    half = own // 2
    packed = jnp.where(lane[:half] < HALF, total[:half], total[half:])
    out[...] = jnp.broadcast_to(packed[None], out.shape)


def apply_kernel(order, field, kernel, out, rows, left, right, sums, tall):
    blocks, half, _ = field.shape
    columns = left.shape[1]
    count = kernel.shape[2]
    spans = [slice(lo, min(lo + SPAN, columns)) for lo in range(0, columns, SPAN)]
    units = [(span, k) for span in spans for k in (0, 2, 1, 3)]
    ready = [0]

    def prepare(span):
        lane = iota((half, LANES), 1)
        while ready[0] * 2 * half < span.stop:
            b = ready[0]
            x = field[order.index(b)]
            turned = pltpu.roll(x, HALF, 1)
            rows[2 * half * b : 2 * half * b + half] = jnp.where(lane < HALF, x, turned)
            rows[2 * half * b + half : 2 * half * (b + 1)] = jnp.where(lane < HALF, turned, x)
            ready[0] += 1
        lane = iota((LANES, LANES), 1)
        for j in range(span.start, span.stop, LANES):
            x = rows[j : j + LANES]
            x = jnp.where(lane < HALF, x, rest_of(x))
            right[j : j + LANES] = x.astype(bf16)

    for span in spans:
        prepare(span)
        for k in range(PARTS):
            x = kernel[k // 2, k % 2, :, span]
            rounded = x.astype(bf16)
            rest = (x - rounded.astype(f32)).astype(bf16)
            x = dot(rounded, right[span]) + dot(rest, right[span])
            tall[k] = x if span.start == 0 else tall[k] + x
    grown = []
    for w in range(2):
        real, imag = tall[2 * w], tall[2 * w + 1]
        real, imag = real + pltpu.roll(real, HALF, 1), imag + pltpu.roll(imag, HALF, 1)
        lane = iota(real.shape, 1)
        crossed = jnp.where(
            (lane & 16) == 0, -pltpu.roll(imag, LANES - 16, 1), pltpu.roll(imag, 16, 1)
        )
        grown.append(real + crossed)
    out[...] = jnp.where((lane & 32) == 0, grown[0], grown[1]).T[:HALF]


def split_kernel(_, kernel, high, low):
    count, columns = kernel.shape[2:]
    cut = columns // 256 * LANES
    for k in range(PARTS):
        for c in range(0, count, 16):
            at = slice(k * count + c, k * count + c + 16)
            for span in (slice(0, cut), slice(cut, columns)):
                x = kernel[k // 2, k % 2, c : c + 16, span]
                high[at, span] = x.astype(bf16)
                x = x - high[at, span].astype(f32)
                low[at, span] = x.astype(bf16)


def adjoint_kernel(order, one, other, mixing, high, low, out, flat, rows):
    count = high.shape[0] // PARTS
    x = one[...] + other[...]
    minus = mixing[0] * x
    for d in range(1, PARTS):
        at = FOCAL * d
        minus = minus + mixing[d] * jnp.concatenate([x[at:], x[:at]], 0)
    upper, lower = minus.astype(bf16), rest_of(minus).astype(bf16)
    columns = flat.shape[1]
    lefts = []
    for w in range(2):
        at = 32 * w
        lefts.append(jnp.concatenate([upper[at : at + 32], lower[at : at + 32]], 0))
        left = []
        for v in (upper, lower):
            left += [v[at + 16 : at + 32], -v[at : at + 16]]
        lefts.append(jnp.concatenate(left, 0))
    for lo in range(0, columns, DSPAN):
        at = slice(lo, min(lo + DSPAN, columns))
        for w in range(2):
            total = None
            for p in range(2):
                left = lefts[2 * w + p]
                base = (2 * w + p) * count
                term = dot(left, high[base : base + count, at])
                term = term[:32] + term[32:] + dot(left[:32], low[base : base + count, at])
                total = term if total is None else total + term
            flat[32 * w : 32 * w + 32, at] = total
        for j in range(at.start, at.stop, LANES):
            block = flat[:, j : j + LANES]
            rows[j : j + LANES] = jnp.concatenate([block, block], 0).T
    blocks, half, _ = out.shape
    lane = iota((half, LANES), 1)
    for b in range(blocks):
        at = 2 * half * b
        out[order.index(b)] = jnp.where(lane < HALF, rows[at : at + half], rows[at + half : at + 2 * half])


def signal_kernel(chunks, pieces, last, direct, out, done, update, wide, out_sems):
    own, focal, samples = done.shape
    total = pieces[0]
    for b in range(1, pieces.shape[0]):
        total = total + pieces[b]
    turned = pltpu.roll(total, HALF, 1)
    half = own // 2
    lane = iota((half, LANES), 1)
    update[:half] = jnp.where(lane < HALF, total, turned)
    update[half:] = jnp.where(lane < HALF, turned, total)
    x = update[...]
    lane = iota(x.shape, 1)
    x = jnp.where(lane < HALF, x, rest_of(x))
    for f in range(focal):
        wide[pl.ds(f, own, stride=focal), :] = jnp.where((lane & 15) == f, x, 0.0)
    backs = []
    for i, (lo, hi) in enumerate(chunks):
        left = wide[lo * focal : hi * focal].astype(bf16)
        value = dot(jnp.concatenate([left, left], 1), last[...])
        done[lo:hi] = direct[lo:hi] - value.reshape(hi - lo, focal, samples)
        backs.append(pltpu.make_async_copy(done.at[lo:hi], out.at[lo:hi], out_sems.at[i]))
        backs[-1].start()
    for copy in backs:
        copy.wait()


def members():
    return [(9 * i) % 32 for i in range(32)]


def call(kernel, outs, ins, out_specs, scratch=(), cost=0, grid=None, limit=32):
    kwargs = {} if grid is None else dict(grid=grid)
    return pl.pallas_call(
        kernel,
        out_shape=outs,
        in_specs=ins,
        out_specs=out_specs,
        scratch_shapes=list(scratch),
        compiler_params=pltpu.CompilerParams(vmem_limit_bytes=limit << 20),
        cost_estimate=pl.CostEstimate(flops=cost, bytes_accessed=cost, transcendentals=0),
        **kwargs,
    )


def local(focusing_plus, direct_field, reflectivity, frequency_bins, focal_onsets, line_offsets):
    own, focal, samples = focusing_plus.shape
    waves, _, block_rows, columns = reflectivity.shape
    blocks = columns // own
    half = own // 2
    assert (waves, focal, own) == (2, FOCAL, LINE)
    chunks = [(0, 16), (16, 40), (40, 64), (64, own)]
    order = members()
    assert sorted(order) == list(range(blocks))
    exchange = functools.partial(
        lax.all_to_all,
        axis_name="blk",
        split_axis=0,
        concat_axis=0,
        tiled=True,
        axis_index_groups=[order],
    )
    shape = jax.ShapeDtypeStruct
    far = functools.partial(pltpu.with_memory_space_constraint, memory_space=pltpu.HBM)

    wide, mixing, last = call(
        functools.partial(spectrum_kernel, ("blk", "cols")),
        [
            pltpu.VMEM((own * focal, LANES), f32),
            pltpu.VMEM((PARTS, HALF, block_rows), f32),
            pltpu.VMEM((4 * HALF, samples), bf16),
        ],
        [ANY] * 4,
        [VMEM] * 3,
        [
            pltpu.SMEM(frequency_bins.shape, jnp.int32),
            pltpu.SMEM(focal_onsets.shape, jnp.int32),
            pltpu.SMEM(line_offsets.shape, jnp.int32),
            pltpu.VMEM((own, focal, samples), f32),
            pltpu.VMEM((samples, LANES), bf16),
            pltpu.SemaphoreType.DMA,
            pltpu.SemaphoreType.DMA((3,)),
        ],
        limit=16,
    )(far(frequency_bins), far(focal_onsets), far(line_offsets), far(focusing_plus))
    copies = call(
        pack_kernel,
        shape((blocks, half, LANES), f32),
        [VMEM, ANY],
        VMEM,
        limit=16,
    )(wide, far(reflectivity))
    field = exchange(copies)

    value = call(
        functools.partial(apply_kernel, order),
        shape((HALF, block_rows), f32),
        [VMEM, VMEM],
        VMEM,
        [
            pltpu.VMEM((columns, LANES), f32),
            pltpu.VMEM((LANES, columns), bf16),
            pltpu.VMEM((columns, LANES), bf16),
            pltpu.VMEM((2, 32, block_rows), f32),
            pltpu.VMEM((4, block_rows, LANES), f32),
        ],
        limit=16,
    )(field, reflectivity)
    value = value + lax.ppermute(value, "cols", [(0, 1), (1, 0), (2, 3), (3, 2)])
    high, low = call(
        split_kernel,
        [pltpu.VMEM((PARTS * block_rows, columns), bf16)] * 2,
        [ANY, VMEM],
        [VMEM] * 2,
        cost=8 << 20,
        limit=16,
    )(value, reflectivity)
    other = lax.ppermute(value, "cols", [(0, 2), (2, 0), (1, 3), (3, 1)])

    partial_update = call(
        functools.partial(adjoint_kernel, order),
        shape((blocks, half, LANES), f32),
        [VMEM] * 5,
        VMEM,
        [pltpu.VMEM((HALF, columns), f32), pltpu.VMEM((columns, LANES), f32)],
    )(value, other, mixing, high, low)
    pieces = exchange(partial_update)

    return call(
        functools.partial(signal_kernel, chunks),
        shape((own, focal, samples), f32),
        [VMEM, VMEM, VMEM],
        ANY,
        [
            pltpu.VMEM((own, focal, samples), f32),
            pltpu.VMEM((own, LANES), f32),
            pltpu.VMEM((own * focal, LANES), f32),
            pltpu.SemaphoreType.DMA((len(chunks),)),
        ],
    )(pieces, last, direct_field)


def solution(mesh):
    return jax.shard_map(
        local,
        mesh=mesh,
        in_specs=(
            P(("cols", "blk"), None, None),
            P(("cols", "blk"), None, None),
            P(None, None, "blk", "cols"),
            P(),
            P(),
            P(),
        ),
        out_specs=P(("cols", "blk"), None, None),
        check_vma=False,
    )
```

```python
import functools
import math

import jax
import jax.numpy as jnp
from jax import lax
from jax.experimental import pallas as pl
from jax.experimental.pallas import tpu as pltpu
from jax.sharding import PartitionSpec as P

LINE = 76
LANES = 128
HALF = 64
FOCAL = 16
PARTS = 4
SPAN = 512
DSPAN = 1280

VMEM = pl.BlockSpec(memory_space=pltpu.VMEM)
SMEM = pl.BlockSpec(memory_space=pltpu.SMEM)
ANY = pl.BlockSpec(memory_space=pl.ANY)
NT = (((1,), (1,)), ((), ()))
NN = (((1,), (0,)), ((), ()))
f32 = jnp.float32
bf16 = jnp.bfloat16


def dot(a, b, dims=NN, precision=None):
    return lax.dot_general(a, b, dims, precision=precision, preferred_element_type=f32)


def iota(shape, dim):
    return lax.broadcasted_iota(jnp.int32, shape, dim)


def rest_of(x):
    return x - x.astype(bf16).astype(f32)


def waves_of(bins, rows, samples, shift=0):
    shape = (rows, samples)
    part = (iota(shape, 0) + shift) & 3
    step = jnp.where(part < 2, bins[0], bins[1])
    phase = (step * iota(shape, 1) + (samples // 4) * (part & 1)) & (samples - 1)
    return jnp.cos(phase.astype(f32) * (2.0 * math.pi / samples))


def repeated(rows, times):
    one = jnp.concatenate(
        [jnp.broadcast_to(rows[k : k + 1], (FOCAL, rows.shape[1])) for k in range(PARTS)], 0
    )
    return jnp.concatenate([one] * times, 0) if times > 1 else one


def fill_tables(axes, waves, bins, focal_onsets, line_offsets, mixing, last):
    samples = last.shape[1]
    lines = mixing.shape[2] // LINE
    block = lax.axis_index(axes[0])
    group = lax.axis_index(axes[1])
    row = iota((FOCAL, samples), 0)
    time = iota((FOCAL, samples), 1)
    focal = jnp.zeros((FOCAL, samples), jnp.int32)
    for f in range(FOCAL):
        focal = jnp.where(row == f, focal_onsets[f], focal)

    def window(line):
        onset = focal + line_offsets[line]
        return jnp.where((time < onset) | (time >= samples - onset), 1.0, 0.0)

    inside = jnp.concatenate([window(block * lines + l) for l in range(lines)], 0).astype(bf16)
    rows = lines * FOCAL
    count = mixing.shape[2]
    same = (iota((HALF, rows), 0) & 15) == (iota((HALF, rows), 1) & 15)
    first = (iota((rows, count), 0) >> 4) * LINE
    column = iota((rows, count), 1)
    spread = jnp.where((column >= first) & (column < first + LINE), 1.0, 0.0).astype(bf16)
    forward = waves * (1.0 / math.sqrt(samples))
    for d in range(PARTS):
        pair = forward * waves_of(bins, 8, samples, d)
        value = dot(repeated(pair, 1).astype(bf16), inside, NT) + dot(
            repeated(rest_of(pair), 1).astype(bf16), inside, NT
        )
        value = jnp.where(same, value, 0.0)
        mixing[d] = dot(value.astype(bf16), spread) + dot(rest_of(value).astype(bf16), spread)
    own = window(group * (line_offsets.shape[0] // 4) + block)
    inverse = repeated(waves, 1) * jnp.concatenate([own] * PARTS, 0)
    high, low = inverse.astype(bf16), rest_of(inverse).astype(bf16)
    last[0:64] = high
    last[64:128] = high
    last[128:192] = low
    last[192:256] = low


def spectrum_kernel(
    axes, bins_in, focal_in, lines_in, signal, wide, mixing, last,
    bins, focal_onsets, line_offsets, held, table, sem, sems,
):
    own, focal, samples = held.shape
    fetches = []
    for i, (source, target) in enumerate(
        [(bins_in, bins), (focal_in, focal_onsets), (lines_in, line_offsets)]
    ):
        fetches.append(pltpu.make_async_copy(source, target, sems.at[i]))
        fetches[-1].start()
    copy = pltpu.make_async_copy(signal, held, sem)
    copy.start()
    for fetch in fetches:
        fetch.wait()
    waves = waves_of(bins, 8, samples)
    forward = waves * (1.0 / math.sqrt(samples))
    table[...] = jnp.concatenate(
        [repeated(forward, 1), repeated(rest_of(forward), 1)], 0
    ).T.astype(bf16)
    fill_tables(axes, waves, bins, focal_onsets, line_offsets, mixing, last)
    both = table[...]
    copy.wait()
    x = held[...].reshape(own * focal, samples)
    rounded = x.astype(bf16)
    wide[...] = dot(rounded, both) + dot((x - rounded.astype(f32)).astype(bf16), both)


def pack_kernel(wide, _, out):
    own = 2 * out.shape[1]
    lane = iota((own, LANES), 1)
    total = jnp.zeros((own, LANES), f32)
    for f in range(FOCAL):
        total = jnp.where((lane & 15) == f, wide[pl.ds(f, own, stride=FOCAL), :], total)
    total = total + pltpu.roll(total, HALF, 1)
    half = own // 2
    packed = jnp.where(lane[:half] < HALF, total[:half], total[half:])
    out[...] = jnp.broadcast_to(packed[None], out.shape)


def apply_kernel(order, field, kernel, out, rows, left, right, sums, tall):
    blocks, half, _ = field.shape
    columns = left.shape[1]
    count = kernel.shape[2]
    spans = [slice(lo, min(lo + SPAN, columns)) for lo in range(0, columns, SPAN)]
    units = [(span, k) for span in spans for k in (0, 2, 1, 3)]
    ready = [0]

    def prepare(span):
        lane = iota((half, LANES), 1)
        while ready[0] * 2 * half < span.stop:
            b = ready[0]
            x = field[order.index(b)]
            turned = pltpu.roll(x, HALF, 1)
            rows[2 * half * b : 2 * half * b + half] = jnp.where(lane < HALF, x, turned)
            rows[2 * half * b + half : 2 * half * (b + 1)] = jnp.where(lane < HALF, turned, x)
            ready[0] += 1
        lane = iota((LANES, LANES), 1)
        for j in range(span.start, span.stop, LANES):
            x = rows[j : j + LANES]
            x = jnp.where(lane < HALF, x, rest_of(x))
            right[j : j + LANES] = x.astype(bf16)

    for span in spans:
        prepare(span)
        for k in range(PARTS):
            x = kernel[k // 2, k % 2, :, span]
            rounded = x.astype(bf16)
            rest = (x - rounded.astype(f32)).astype(bf16)
            x = dot(rounded, right[span]) + dot(rest, right[span])
            tall[k] = x if span.start == 0 else tall[k] + x
    grown = []
    for w in range(2):
        real, imag = tall[2 * w], tall[2 * w + 1]
        real, imag = real + pltpu.roll(real, HALF, 1), imag + pltpu.roll(imag, HALF, 1)
        lane = iota(real.shape, 1)
        crossed = jnp.where(
            (lane & 16) == 0, -pltpu.roll(imag, LANES - 16, 1), pltpu.roll(imag, 16, 1)
        )
        grown.append(real + crossed)
    value = jnp.where((lane & 32) == 0, grown[0], grown[1])
    short = out.shape[0]
    out[...] = jnp.where(lane[:short] < HALF, value[:short], value[short:])


def split_kernel(_, kernel, high, low):
    count, columns = kernel.shape[2:]
    cut = columns // 256 * LANES
    for k in range(PARTS):
        for c in range(0, count, 16):
            at = slice(k * count + c, k * count + c + 16)
            for span in (slice(0, cut), slice(cut, columns)):
                x = kernel[k // 2, k % 2, c : c + 16, span]
                high[at, span] = x.astype(bf16)
                x = x - high[at, span].astype(f32)
                low[at, span] = x.astype(bf16)


def adjoint_kernel(order, one, other, mixing, high, low, out, flat, rows):
    count = high.shape[0] // PARTS
    x = one[...] + other[...]
    turned = pltpu.roll(x, HALF, 1)
    low_half = iota(x.shape, 1) < HALF
    x = jnp.concatenate([jnp.where(low_half, x, turned), jnp.where(low_half, turned, x)], 0)
    x = x.T[:HALF]
    minus = mixing[0] * x
    for d in range(1, PARTS):
        at = FOCAL * d
        minus = minus + mixing[d] * jnp.concatenate([x[at:], x[:at]], 0)
    upper, lower = minus.astype(bf16), rest_of(minus).astype(bf16)
    columns = flat.shape[1]
    lefts = []
    for w in range(2):
        at = 32 * w
        lefts.append(jnp.concatenate([upper[at : at + 32], lower[at : at + 32]], 0))
        left = []
        for v in (upper, lower):
            left += [v[at + 16 : at + 32], -v[at : at + 16]]
        lefts.append(jnp.concatenate(left, 0))
    for lo in range(0, columns, DSPAN):
        at = slice(lo, min(lo + DSPAN, columns))
        for w in range(2):
            total = None
            for p in range(2):
                left = lefts[2 * w + p]
                base = (2 * w + p) * count
                term = dot(left, high[base : base + count, at])
                term = term[:32] + term[32:] + dot(left[:32], low[base : base + count, at])
                total = term if total is None else total + term
            flat[32 * w : 32 * w + 32, at] = total
        for j in range(at.start, at.stop, LANES):
            block = flat[:, j : j + LANES]
            rows[j : j + LANES] = jnp.concatenate([block, block], 0).T
    blocks, half, _ = out.shape
    lane = iota((half, LANES), 1)
    for b in range(blocks):
        at = 2 * half * b
        out[order.index(b)] = jnp.where(lane < HALF, rows[at : at + half], rows[at + half : at + 2 * half])


def signal_kernel(chunks, pieces, last, direct, out, done, update, wide, out_sems):
    own, focal, samples = done.shape
    total = pieces[0]
    for b in range(1, pieces.shape[0]):
        total = total + pieces[b]
    turned = pltpu.roll(total, HALF, 1)
    half = own // 2
    lane = iota((half, LANES), 1)
    update[:half] = jnp.where(lane < HALF, total, turned)
    update[half:] = jnp.where(lane < HALF, turned, total)
    x = update[...]
    lane = iota(x.shape, 1)
    x = jnp.where(lane < HALF, x, rest_of(x))
    for f in range(focal):
        wide[pl.ds(f, own, stride=focal), :] = jnp.where((lane & 15) == f, x, 0.0)
    backs = []
    for i, (lo, hi) in enumerate(chunks):
        left = wide[lo * focal : hi * focal].astype(bf16)
        value = dot(jnp.concatenate([left, left], 1), last[...])
        done[lo:hi] = direct[lo:hi] - value.reshape(hi - lo, focal, samples)
        backs.append(pltpu.make_async_copy(done.at[lo:hi], out.at[lo:hi], out_sems.at[i]))
        backs[-1].start()
    for copy in backs:
        copy.wait()


def members():
    return [(9 * i) % 32 for i in range(32)]


def call(kernel, outs, ins, out_specs, scratch=(), cost=0, grid=None, limit=32):
    kwargs = {} if grid is None else dict(grid=grid)
    return pl.pallas_call(
        kernel,
        out_shape=outs,
        in_specs=ins,
        out_specs=out_specs,
        scratch_shapes=list(scratch),
        compiler_params=pltpu.CompilerParams(vmem_limit_bytes=limit << 20),
        cost_estimate=pl.CostEstimate(flops=cost, bytes_accessed=cost, transcendentals=0),
        **kwargs,
    )


def local(focusing_plus, direct_field, reflectivity, frequency_bins, focal_onsets, line_offsets):
    own, focal, samples = focusing_plus.shape
    waves, _, block_rows, columns = reflectivity.shape
    blocks = columns // own
    half = own // 2
    assert (waves, focal, own) == (2, FOCAL, LINE)
    chunks = [(0, 16), (16, 40), (40, 64), (64, own)]
    order = members()
    assert sorted(order) == list(range(blocks))
    exchange = functools.partial(
        lax.all_to_all,
        axis_name="blk",
        split_axis=0,
        concat_axis=0,
        tiled=True,
        axis_index_groups=[order],
    )
    shape = jax.ShapeDtypeStruct
    far = functools.partial(pltpu.with_memory_space_constraint, memory_space=pltpu.HBM)

    wide, mixing, last = call(
        functools.partial(spectrum_kernel, ("blk", "cols")),
        [
            pltpu.VMEM((own * focal, LANES), f32),
            pltpu.VMEM((PARTS, HALF, block_rows), f32),
            pltpu.VMEM((4 * HALF, samples), bf16),
        ],
        [ANY] * 4,
        [VMEM] * 3,
        [
            pltpu.SMEM(frequency_bins.shape, jnp.int32),
            pltpu.SMEM(focal_onsets.shape, jnp.int32),
            pltpu.SMEM(line_offsets.shape, jnp.int32),
            pltpu.VMEM((own, focal, samples), f32),
            pltpu.VMEM((samples, LANES), bf16),
            pltpu.SemaphoreType.DMA,
            pltpu.SemaphoreType.DMA((3,)),
        ],
        limit=16,
    )(far(frequency_bins), far(focal_onsets), far(line_offsets), far(focusing_plus))
    copies = call(
        pack_kernel,
        shape((blocks, half, LANES), f32),
        [VMEM, ANY],
        VMEM,
        limit=16,
    )(wide, far(reflectivity))
    field = exchange(copies)

    value = call(
        functools.partial(apply_kernel, order),
        shape((block_rows // 2, LANES), f32),
        [VMEM, VMEM],
        VMEM,
        [
            pltpu.VMEM((columns, LANES), f32),
            pltpu.VMEM((LANES, columns), bf16),
            pltpu.VMEM((columns, LANES), bf16),
            pltpu.VMEM((2, 32, block_rows), f32),
            pltpu.VMEM((4, block_rows, LANES), f32),
        ],
        limit=16,
    )(field, reflectivity)
    value = value + lax.ppermute(value, "cols", [(0, 1), (1, 0), (2, 3), (3, 2)])
    high, low = call(
        split_kernel,
        [pltpu.VMEM((PARTS * block_rows, columns), bf16)] * 2,
        [ANY, VMEM],
        [VMEM] * 2,
        cost=8 << 20,
        limit=16,
    )(value, reflectivity)
    other = lax.ppermute(value, "cols", [(0, 2), (2, 0), (1, 3), (3, 1)])

    partial_update = call(
        functools.partial(adjoint_kernel, order),
        shape((blocks, half, LANES), f32),
        [VMEM] * 5,
        VMEM,
        [pltpu.VMEM((HALF, columns), f32), pltpu.VMEM((columns, LANES), f32)],
    )(value, other, mixing, high, low)
    pieces = exchange(partial_update)

    return call(
        functools.partial(signal_kernel, chunks),
        shape((own, focal, samples), f32),
        [VMEM, VMEM, VMEM],
        ANY,
        [
            pltpu.VMEM((own, focal, samples), f32),
            pltpu.VMEM((own, LANES), f32),
            pltpu.VMEM((own * focal, LANES), f32),
            pltpu.SemaphoreType.DMA((len(chunks),)),
        ],
    )(pieces, last, direct_field)


def solution(mesh):
    return jax.shard_map(
        local,
        mesh=mesh,
        in_specs=(
            P(("cols", "blk"), None, None),
            P(("cols", "blk"), None, None),
            P(None, None, "blk", "cols"),
            P(),
            P(),
            P(),
        ),
        out_specs=P(("cols", "blk"), None, None),
        check_vma=False,
    )
```

```python
import functools
import math

import jax
import jax.numpy as jnp
from jax import lax
from jax.experimental import pallas as pl
from jax.experimental.pallas import tpu as pltpu
from jax.sharding import PartitionSpec as P

LINE = 76
LANES = 128
HALF = 64
FOCAL = 16
PARTS = 4
SPAN = 512
DSPAN = 1280

VMEM = pl.BlockSpec(memory_space=pltpu.VMEM)
SMEM = pl.BlockSpec(memory_space=pltpu.SMEM)
ANY = pl.BlockSpec(memory_space=pl.ANY)
NT = (((1,), (1,)), ((), ()))
NN = (((1,), (0,)), ((), ()))
f32 = jnp.float32
bf16 = jnp.bfloat16


def dot(a, b, dims=NN, precision=None):
    return lax.dot_general(a, b, dims, precision=precision, preferred_element_type=f32)


def iota(shape, dim):
    return lax.broadcasted_iota(jnp.int32, shape, dim)


def rest_of(x):
    return x - x.astype(bf16).astype(f32)


def waves_of(bins, rows, samples, shift=0):
    shape = (rows, samples)
    part = (iota(shape, 0) + shift) & 3
    step = jnp.where(part < 2, bins[0], bins[1])
    phase = (step * iota(shape, 1) + (samples // 4) * (part & 1)) & (samples - 1)
    return jnp.cos(phase.astype(f32) * (2.0 * math.pi / samples))


def repeated(rows, times):
    one = jnp.concatenate(
        [jnp.broadcast_to(rows[k : k + 1], (FOCAL, rows.shape[1])) for k in range(PARTS)], 0
    )
    return jnp.concatenate([one] * times, 0) if times > 1 else one


def fill_tables(axes, waves, bins, focal_onsets, line_offsets, mixing, last):
    samples = last.shape[1]
    lines = mixing.shape[2] // LINE
    block = lax.axis_index(axes[0])
    group = lax.axis_index(axes[1])
    row = iota((FOCAL, samples), 0)
    time = iota((FOCAL, samples), 1)
    focal = jnp.zeros((FOCAL, samples), jnp.int32)
    for f in range(FOCAL):
        focal = jnp.where(row == f, focal_onsets[f], focal)

    def window(line):
        onset = focal + line_offsets[line]
        return jnp.where((time < onset) | (time >= samples - onset), 1.0, 0.0)

    inside = jnp.concatenate([window(block * lines + l) for l in range(lines)], 0).astype(bf16)
    rows = lines * FOCAL
    count = mixing.shape[2]
    same = (iota((HALF, rows), 0) & 15) == (iota((HALF, rows), 1) & 15)
    first = (iota((rows, count), 0) >> 4) * LINE
    column = iota((rows, count), 1)
    spread = jnp.where((column >= first) & (column < first + LINE), 1.0, 0.0).astype(bf16)
    forward = waves * (1.0 / math.sqrt(samples))
    for d in range(PARTS):
        pair = forward * waves_of(bins, 8, samples, d)
        value = dot(repeated(pair, 1).astype(bf16), inside, NT) + dot(
            repeated(rest_of(pair), 1).astype(bf16), inside, NT
        )
        value = jnp.where(same, value, 0.0)
        mixing[d] = dot(value.astype(bf16), spread) + dot(rest_of(value).astype(bf16), spread)
    own = window(group * (line_offsets.shape[0] // 4) + block)
    inverse = repeated(waves, 1) * jnp.concatenate([own] * PARTS, 0)
    high, low = inverse.astype(bf16), rest_of(inverse).astype(bf16)
    last[0:64] = high
    last[64:128] = high
    last[128:192] = low
    last[192:256] = low


def spectrum_kernel(
    axes, bins_in, focal_in, lines_in, signal, wide, mixing, last,
    bins, focal_onsets, line_offsets, held, table, sem, sems,
):
    own, focal, samples = held.shape
    fetches = []
    for i, (source, target) in enumerate(
        [(bins_in, bins), (focal_in, focal_onsets), (lines_in, line_offsets)]
    ):
        fetches.append(pltpu.make_async_copy(source, target, sems.at[i]))
        fetches[-1].start()
    copy = pltpu.make_async_copy(signal, held, sem)
    copy.start()
    for fetch in fetches:
        fetch.wait()
    waves = waves_of(bins, 8, samples)
    forward = waves * (1.0 / math.sqrt(samples))
    table[...] = jnp.concatenate(
        [repeated(forward, 1), repeated(rest_of(forward), 1)], 0
    ).T.astype(bf16)
    fill_tables(axes, waves, bins, focal_onsets, line_offsets, mixing, last)
    both = table[...]
    copy.wait()
    x = held[...].reshape(own * focal, samples)
    rounded = x.astype(bf16)
    wide[...] = dot(rounded, both) + dot((x - rounded.astype(f32)).astype(bf16), both)


def pack_kernel(wide, _, out):
    own = 2 * out.shape[1]
    lane = iota((own, LANES), 1)
    total = jnp.zeros((own, LANES), f32)
    for f in range(FOCAL):
        total = jnp.where((lane & 15) == f, wide[pl.ds(f, own, stride=FOCAL), :], total)
    total = total + pltpu.roll(total, HALF, 1)
    half = own // 2
    packed = jnp.where(lane[:half] < HALF, total[:half], total[half:])
    out[...] = jnp.broadcast_to(packed[None], out.shape)


def apply_kernel(order, field, kernel, out, rows, left, right, sums, tall):
    blocks, half, _ = field.shape
    columns = left.shape[1]
    count = kernel.shape[2]
    spans = [slice(lo, min(lo + SPAN, columns)) for lo in range(0, columns, SPAN)]
    units = [(span, k) for span in spans for k in (0, 2, 1, 3)]
    ready = [0]

    def prepare(span):
        lane = iota((half, LANES), 1)
        while ready[0] * 2 * half < span.stop:
            b = ready[0]
            x = field[order.index(b)]
            turned = pltpu.roll(x, HALF, 1)
            rows[2 * half * b : 2 * half * b + half] = jnp.where(lane < HALF, x, turned)
            rows[2 * half * b + half : 2 * half * (b + 1)] = jnp.where(lane < HALF, turned, x)
            ready[0] += 1
        lane = iota((LANES, LANES), 1)
        for j in range(span.start, span.stop, LANES):
            x = rows[j : j + LANES]
            x = jnp.where(lane < HALF, x, rest_of(x))
            right[j : j + LANES] = x.astype(bf16)

    for span in spans:
        prepare(span)
        for k in range(PARTS):
            x = kernel[k // 2, k % 2, :, span]
            rounded = x.astype(bf16)
            rest = (x - rounded.astype(f32)).astype(bf16)
            x = dot(rounded, right[span]) + dot(rest, right[span])
            tall[k] = x if span.start == 0 else tall[k] + x
    grown = []
    for w in range(2):
        real, imag = tall[2 * w], tall[2 * w + 1]
        real, imag = real + pltpu.roll(real, HALF, 1), imag + pltpu.roll(imag, HALF, 1)
        lane = iota(real.shape, 1)
        crossed = jnp.where(
            (lane & 16) == 0, -pltpu.roll(imag, LANES - 16, 1), pltpu.roll(imag, 16, 1)
        )
        grown.append(real + crossed)
    value = jnp.where((lane & 32) == 0, grown[0], grown[1])
    short = out.shape[0]
    out[...] = jnp.where(lane[:short] < HALF, value[:short], value[short:])


def split_kernel(_, kernel, high, low):
    count, columns = kernel.shape[2:]
    cut = columns // 256 * LANES
    for k in range(PARTS):
        for c in range(0, count, 16):
            at = slice(k * count + c, k * count + c + 16)
            for span in (slice(0, cut), slice(cut, columns)):
                x = kernel[k // 2, k % 2, c : c + 16, span]
                high[at, span] = x.astype(bf16)
                x = x - high[at, span].astype(f32)
                low[at, span] = x.astype(bf16)


def adjoint_kernel(order, one, other, mixing, high, low, out, flat, rows):
    count = high.shape[0] // PARTS
    x = one[...] + other[...]
    turned = pltpu.roll(x, HALF, 1)
    low_half = iota(x.shape, 1) < HALF
    x = jnp.concatenate([jnp.where(low_half, x, turned), jnp.where(low_half, turned, x)], 0)
    x = x.T[:HALF]
    minus = mixing[0] * x
    for d in range(1, PARTS):
        at = FOCAL * d
        minus = minus + mixing[d] * jnp.concatenate([x[at:], x[:at]], 0)
    upper, lower = minus.astype(bf16), rest_of(minus).astype(bf16)
    columns = flat.shape[1]
    lefts = []
    for w in range(2):
        at = 32 * w
        lefts.append(jnp.concatenate([upper[at : at + 32], lower[at : at + 32]], 0))
        left = []
        for v in (upper, lower):
            left += [v[at + 16 : at + 32], -v[at : at + 16]]
        lefts.append(jnp.concatenate(left, 0))
    for lo in range(0, columns, DSPAN):
        at = slice(lo, min(lo + DSPAN, columns))
        for w in range(2):
            total = None
            for p in range(2):
                left = lefts[2 * w + p]
                base = (2 * w + p) * count
                term = dot(left, high[base : base + count, at])
                term = term[:32] + term[32:] + dot(left[:32], low[base : base + count, at])
                total = term if total is None else total + term
            flat[32 * w : 32 * w + 32, at] = total
        for j in range(at.start, at.stop, LANES):
            block = flat[:, j : j + LANES]
            rows[j : j + LANES] = jnp.concatenate([block, block], 0).T
    blocks, half, _ = out.shape
    lane = iota((half, LANES), 1)
    for b in range(blocks):
        at = 2 * half * b
        out[order.index(b)] = jnp.where(lane < HALF, rows[at : at + half], rows[at + half : at + 2 * half])


def signal_kernel(chunks, pieces, last, direct, out, done, update, wide, out_sems):
    own, focal, samples = done.shape
    total = pieces[0]
    for b in range(1, pieces.shape[0]):
        total = total + pieces[b]
    turned = pltpu.roll(total, HALF, 1)
    half = own // 2
    lane = iota((half, LANES), 1)
    update[:half] = jnp.where(lane < HALF, total, turned)
    update[half:] = jnp.where(lane < HALF, turned, total)
    x = update[...]
    lane = iota(x.shape, 1)
    x = jnp.where(lane < HALF, x, rest_of(x))
    for f in range(focal):
        wide[pl.ds(f, own, stride=focal), :] = jnp.where((lane & 15) == f, x, 0.0)
    backs = []
    for i, (lo, hi) in enumerate(chunks):
        left = wide[lo * focal : hi * focal].astype(bf16)
        value = dot(jnp.concatenate([left, left], 1), last[...])
        done[lo:hi] = direct[lo:hi] - value.reshape(hi - lo, focal, samples)
        backs.append(pltpu.make_async_copy(done.at[lo:hi], out.at[lo:hi], out_sems.at[i]))
        backs[-1].start()
    for copy in backs:
        copy.wait()


def members():
    return [(9 * i) % 32 for i in range(32)]


def call(kernel, outs, ins, out_specs, scratch=(), cost=0, grid=None, limit=32):
    kwargs = {} if grid is None else dict(grid=grid)
    return pl.pallas_call(
        kernel,
        out_shape=outs,
        in_specs=ins,
        out_specs=out_specs,
        scratch_shapes=list(scratch),
        compiler_params=pltpu.CompilerParams(vmem_limit_bytes=limit << 20),
        cost_estimate=pl.CostEstimate(flops=cost, bytes_accessed=cost, transcendentals=0),
        **kwargs,
    )


def local(focusing_plus, direct_field, reflectivity, frequency_bins, focal_onsets, line_offsets):
    own, focal, samples = focusing_plus.shape
    waves, _, block_rows, columns = reflectivity.shape
    blocks = columns // own
    half = own // 2
    assert (waves, focal, own) == (2, FOCAL, LINE)
    chunks = [(0, 16), (16, 44), (44, own)]
    order = members()
    assert sorted(order) == list(range(blocks))
    exchange = functools.partial(
        lax.all_to_all,
        axis_name="blk",
        split_axis=0,
        concat_axis=0,
        tiled=True,
        axis_index_groups=[order],
    )
    shape = jax.ShapeDtypeStruct
    far = functools.partial(pltpu.with_memory_space_constraint, memory_space=pltpu.HBM)

    wide, mixing, last = call(
        functools.partial(spectrum_kernel, ("blk", "cols")),
        [
            pltpu.VMEM((own * focal, LANES), f32),
            pltpu.VMEM((PARTS, HALF, block_rows), f32),
            pltpu.VMEM((4 * HALF, samples), bf16),
        ],
        [ANY] * 4,
        [VMEM] * 3,
        [
            pltpu.SMEM(frequency_bins.shape, jnp.int32),
            pltpu.SMEM(focal_onsets.shape, jnp.int32),
            pltpu.SMEM(line_offsets.shape, jnp.int32),
            pltpu.VMEM((own, focal, samples), f32),
            pltpu.VMEM((samples, LANES), bf16),
            pltpu.SemaphoreType.DMA,
            pltpu.SemaphoreType.DMA((3,)),
        ],
        limit=16,
    )(far(frequency_bins), far(focal_onsets), far(line_offsets), far(focusing_plus))
    copies = call(
        pack_kernel,
        shape((blocks, half, LANES), f32),
        [VMEM, ANY],
        VMEM,
        limit=16,
    )(wide, far(reflectivity))
    field = exchange(copies)

    value = call(
        functools.partial(apply_kernel, order),
        shape((block_rows // 2, LANES), f32),
        [VMEM, VMEM],
        VMEM,
        [
            pltpu.VMEM((columns, LANES), f32),
            pltpu.VMEM((LANES, columns), bf16),
            pltpu.VMEM((columns, LANES), bf16),
            pltpu.VMEM((2, 32, block_rows), f32),
            pltpu.VMEM((4, block_rows, LANES), f32),
        ],
        limit=16,
    )(field, reflectivity)
    value = value + lax.ppermute(value, "cols", [(0, 1), (1, 0), (2, 3), (3, 2)])
    high, low = call(
        split_kernel,
        [pltpu.VMEM((PARTS * block_rows, columns), bf16)] * 2,
        [ANY, VMEM],
        [VMEM] * 2,
        cost=8 << 20,
        limit=16,
    )(value, reflectivity)
    other = lax.ppermute(value, "cols", [(0, 2), (2, 0), (1, 3), (3, 1)])

    partial_update = call(
        functools.partial(adjoint_kernel, order),
        shape((blocks, half, LANES), f32),
        [VMEM] * 5,
        VMEM,
        [pltpu.VMEM((HALF, columns), f32), pltpu.VMEM((columns, LANES), f32)],
    )(value, other, mixing, high, low)
    pieces = exchange(partial_update)

    return call(
        functools.partial(signal_kernel, chunks),
        shape((own, focal, samples), f32),
        [VMEM, VMEM, VMEM],
        ANY,
        [
            pltpu.VMEM((own, focal, samples), f32),
            pltpu.VMEM((own, LANES), f32),
            pltpu.VMEM((own * focal, LANES), f32),
            pltpu.SemaphoreType.DMA((len(chunks),)),
        ],
    )(pieces, last, direct_field)


def solution(mesh):
    return jax.shard_map(
        local,
        mesh=mesh,
        in_specs=(
            P(("cols", "blk"), None, None),
            P(("cols", "blk"), None, None),
            P(None, None, "blk", "cols"),
            P(),
            P(),
            P(),
        ),
        out_specs=P(("cols", "blk"), None, None),
        check_vma=False,
    )
```
